128 devices in a mesh: bath: 32 (over x, y, z_hi), imp: 4 (over z_lo, core).
Axes of the slice: x: 4, y: 4, z: 4 (z_hi: 2, z_lo: 2; z = z_hi * 2 + z_lo), core: 2. Of those that a mesh axis runs over, the one named last changes fastest.
Arguments:
- psi: bfloat16 [32, 1024, 2048], P('bath', 'imp'), may hold values from -6 to 6
- h_imp: bfloat16 [1024, 1024], P(None, 'imp'), may hold values from -0.1875 to 0.1875
- hops: bfloat16 [2, 5, 1024, 1024], P(None, None, None, 'imp'), may hold values from -0.3125 to 0.3125
- patterns: int32 [2, 5, 8, 8], replicated, may hold values from 0 to 1, as said below
- signs: int32 [5, 32, 8], P(None, 'bath'), may hold values 0 or 1
- bath_energy: float32 [32], P('bath'), may hold values from -2 to 2
Outputs:
- applied: float32 [32, 1024, 2048], P('bath', 'imp')
The draws below stay inside these ranges and needn't reach their ends.
Inputs may be any that keep to these rules, and one draw needn't show every extreme that they name: `patterns`: each hybridization operator has exactly 24 nonzero blocks.
All inputs are finite; a program needn't handle non-finite values. No bound on the sum of `signs` on one device may be relied on, other than what follows from the above.
Results may differ from the reference program's by a relative error of at most 0.0003.
Values may be sent and summed in bfloat16 or wider, within the bound.
A program may use at most 128 MiB of HBM per device.

```python
import jax
import jax.numpy as jnp
from jax import lax

NBLK = 8
NZ = 24
REST = 2048
IMPS = 1024
NBS = 32
BITS = 5


def draw_patterns(key, part):
    keys = jax.random.split(jax.random.fold_in(key, 17), 2 * BITS)
    orders = jax.vmap(lambda one_key: jax.random.permutation(one_key, NBLK * NBLK))(keys)
    chosen = (orders < NZ).astype(jnp.int32)
    return chosen.reshape(2, BITS, NBLK, NBLK)


def place_ends(values, rng, least, top_value):
    longest = values.shape.index(max(values.shape))
    spots = []
    for shift in (0, 1):
        where = [jax.random.randint(jax.random.fold_in(rng, axis), (), 0, length) for axis, length in enumerate(values.shape)]
        where[longest] = (where[longest] + shift) % values.shape[longest]
        spots.append(tuple(where))
    return values.at[spots[0]].set(least).at[spots[1]].set(top_value)


def shard_levels(rng, extent, shards, least, largest):
    factor_of, own = 1.0, jax.random.fold_in(rng, 6)
    for axis_at, parts in shards:
        steps = jnp.exp(jax.random.uniform(jax.random.fold_in(own, axis_at), (parts,), jnp.float32, least / len(shards), largest / len(shards)))
        factor_of = factor_of * jnp.repeat(steps, extent[axis_at] // parts).reshape([-1 if axis == axis_at else 1 for axis in range(len(extent))])
    return factor_of


def gaussian(key, shape, scale, most, shards=(), held_as=jnp.bfloat16):
    entries = jax.random.normal(key, shape, jnp.float32) * scale
    if len(shards) > 0:
        entries = shard_levels(key, shape, shards, -0.22, 0.18) * entries
    return jnp.clip(entries, min=-most, max=most).astype(held_as)


def setup_inputs(seed: int = 0) -> dict:
    key_of = jax.random.split(jax.random.key(seed), 7)
    psi = gaussian(key_of[0], (NBS, IMPS, REST), 1.0, 6.0, ((0, 32), (1, 4)))
    h_imp = gaussian(key_of[1], (IMPS, IMPS), IMPS ** -0.5, 0.1875, ((1, 4),))
    hops = gaussian(key_of[2], (2, BITS, IMPS, IMPS), (IMPS * NZ // (NBLK * NBLK)) ** -0.5, 0.3125, ((3, 4),))
    patterns = draw_patterns(jax.random.fold_in(key_of[6], 71), 0)
    signs = place_ends((jax.random.randint(key_of[4], (BITS, NBS, NBLK), 0, 2) < 1).astype(jnp.int32), jax.random.fold_in(key_of[4], 1), 0, 1)
    bath_energy = jnp.clip(jax.random.uniform(key_of[5], (NBS,), jnp.float32, -2.0, 2.0) * shard_levels(key_of[5], (NBS,), ((0, 32),), -0.4, 0.0), -2.0, 2.0)
    return dict(psi=psi, h_imp=h_imp, hops=hops, patterns=patterns, signs=signs, bath_energy=bath_energy)


def reference(psi, h_imp, hops, patterns, signs, bath_energy):
    imps = psi.shape[1]
    blk = imps // NBLK
    block_mask = jnp.repeat(jnp.repeat(patterns, blk, axis=2), blk, axis=3).astype(jnp.float32)
    masked = hops.astype(jnp.float32) * block_mask
    himp_f = h_imp.astype(jnp.float32)

    def one_state(state):
        own = psi[state].astype(jnp.float32)
        total = jnp.dot(himp_f, own, precision=lax.Precision.HIGHEST, preferred_element_type=jnp.float32)
        for level in range(BITS):
            side = jnp.bitwise_and(jnp.right_shift(state, level), 1).astype(jnp.int32)
            partner_index = jnp.bitwise_xor(state, 1 << level).astype(jnp.int32)
            partner = psi[partner_index].astype(jnp.float32)
            matrix = masked[side, level]
            factor = jnp.repeat(1.0 - 2.0 * signs[level, state].astype(jnp.float32), blk)
            product = jnp.dot(matrix, partner, precision=lax.Precision.HIGHEST, preferred_element_type=jnp.float32)
            total = total + factor[:, None] * product
        return total + bath_energy[state] * own

    return lax.map(one_state, jnp.arange(psi.shape[0], dtype=jnp.int32))
```

```python
import jax
import jax.numpy as jnp
from jax import lax
from jax.experimental import pallas as pl
from jax.experimental.pallas import tpu as pltpu
from jax.sharding import PartitionSpec as P

MESH = pl.DeviceIdType.MESH
CHUNKS = 4
LEAST = 1e-30
TOP = 32767.0


def flip(index, bit):
    return index + bit - 2 * bit * ((index // bit) % 2)


def kernel(
    psi, h_imp, hops, patterns, signs, energy, out,
    raw, weights, amps, kept, other, coded, scales, coded_in, scales_in, stage,
    own_sem, mat_sem, near_send, near_recv, pair_send, pair_recv, pass_send, pass_recv,
    sum_send, sum_recv, end_send, end_recv, op_send, op_recv,
):
    bath, imp = lax.axis_index("bath"), lax.axis_index("imp")
    z_lo, core = imp // 2, imp % 2
    side = [(bath // (1 << level)) % 2 for level in range(5)]
    rows, rest = psi.shape
    half = rest // 2
    width = half // CHUNKS
    chip_rows = 2 * rows
    blk = 128

    sibling = (bath, flip(imp, 1))
    across = (bath, flip(imp, 2))
    near = [
        [(flip(bath, 2), z_lo * 2 + q) for q in range(2)],
        [(flip(bath, 8), z_lo * 2 + q) for q in range(2)],
        [(flip(bath, 1), (1 - z_lo) * 2 + q) for q in range(2)],
    ]
    onward = [(flip(flip(bath, 2), 4), imp), (flip(flip(bath, 8), 16), imp)]
    near_slot = (1, 3, 5)
    onward_slot = (2, 4)

    def slot_rows(slot, q):
        return pl.ds(pl.multiple_of(slot * chip_rows + q * rows, rows), rows)

    def columns(q, j):
        return pl.ds(pl.multiple_of(q * half + j * width, 128), width)

    def remote(src, dst, send, recv, device):
        return pltpu.make_async_remote_copy(
            src_ref=src, dst_ref=dst, send_sem=send, recv_sem=recv, device_id=device, device_id_type=MESH
        )

    own = [
        pltpu.make_async_copy(psi.at[:, columns(core, j)], amps.at[j, slot_rows(0, core), :], own_sem.at[j])
        for j in range(CHUNKS)
    ]
    mats = [pltpu.make_async_copy(h_imp, weights.at[:, slot_rows(0, core)], mat_sem.at[0])]
    for level in range(1, 5):
        mats.append(pltpu.make_async_copy(hops.at[side[level], level], raw.at[level, core], mat_sem.at[level]))
    for copy in mats + own:
        copy.start()

    barrier = pltpu.get_barrier_semaphore()
    peers = [sibling, across] + near[0] + near[1] + near[2] + onward
    for peer in peers:
        pl.semaphore_signal(barrier, inc=1, device_id=peer, device_id_type=MESH)
    pl.semaphore_wait(barrier, len(peers))

    def near_copy(a, j, q):
        return remote(
            psi.at[:, columns(q, j)],
            amps.at[j, slot_rows(near_slot[a], core), :],
            near_send.at[a, j, q],
            near_recv.at[a, j, core],
            near[a][q],
        )

    def near_wait(a, j):
        for q in range(2):
            remote(
                psi.at[:, columns(q, j)],
                amps.at[j, slot_rows(near_slot[a], q), :],
                near_send.at[a, j, q],
                near_recv.at[a, j, q],
                near[a][q],
            ).wait_recv()

    def pair_copy(j):
        return remote(
            psi.at[:, columns(1 - core, j)],
            amps.at[j, slot_rows(0, core), :],
            pair_send.at[j],
            pair_recv.at[j],
            sibling,
        )

    def pair_wait(j):
        remote(
            psi.at[:, columns(core, j)],
            amps.at[j, slot_rows(0, 1 - core), :],
            pair_send.at[j],
            pair_recv.at[j],
            sibling,
        ).wait_recv()

    def pass_copy(a, j):
        src = pl.ds(near_slot[a] * chip_rows, chip_rows)
        dst = pl.ds(onward_slot[a] * chip_rows, chip_rows)
        return remote(
            amps.at[j, src, :], amps.at[j, dst, :], pass_send.at[a, j], pass_recv.at[a, j], onward[a]
        )

    def sum_copy(j):
        return (
            remote(coded.at[j], coded_in.at[j], sum_send.at[j, 0], sum_recv.at[j, 0], across),
            remote(scales.at[j], scales_in.at[j], sum_send.at[j, 1], sum_recv.at[j, 1], across),
        )

    def end_copy(j):
        return remote(stage.at[j], out.at[:, columns(core, j)], end_send.at[j], end_recv.at[j], sibling)

    def end_wait(j):
        remote(
            stage.at[j], out.at[:, columns(1 - core, j)], end_send.at[j], end_recv.at[j], sibling
        ).wait_recv()

    op0 = remote(hops.at[side[0], 0], raw.at[0, core], op_send.at[0], op_recv.at[0], across)
    op0_on = remote(raw.at[0, core], raw.at[0, core], op_send.at[6], op_recv.at[6], sibling)
    ops = [
        remote(h_imp, weights.at[:, slot_rows(0, core)], op_send.at[5], op_recv.at[5], sibling)
    ]
    for level in range(1, 5):
        ops.append(
            remote(
                hops.at[side[level], level], raw.at[level, core], op_send.at[level], op_recv.at[level], sibling
            )
        )

    for j in range(CHUNKS):
        for q in range(2):
            for a in range(3):
                near_copy(a, j, q).start()
        if j == 0:
            op0.start()
            pair_copy(0).start()
            for copy in ops:
                copy.start()
        else:
            pair_copy(j).start()

    def mask(level, slot, q, from_z):
        def block(p, carry):
            sign = (1 - 2 * signs[level, 0, p]).astype(jnp.float32)
            for k in range(rows // blk):
                keep = patterns[side[level], level, p, from_z * 4 + q * 2 + k].astype(jnp.float32)
                factor = jnp.full((blk, blk), keep * sign, jnp.float32).astype(jnp.bfloat16)
                at = pl.ds(pl.multiple_of(p * blk, blk), blk)
                to = pl.ds(pl.multiple_of(slot * chip_rows + q * rows + k * blk, blk), blk)
                weights[at, to] = raw[level, q, at, k * blk : (k + 1) * blk] * factor
            return carry

        lax.fori_loop(0, 8, block, 0)

    for level in range(1, 5):
        mats[level].wait()
        mask(level, level, core, z_lo)
    for level in range(1, 5):
        ops[level].wait_recv()
        mask(level, level, 1 - core, z_lo)
    mats[0].wait()
    ops[0].wait_recv()
    op0.wait_recv()
    op0_on.start()
    mask(0, 5, core, 1 - z_lo)

    def forward(j):
        for a in range(2):
            near_wait(a, j)
            pass_copy(a, j).start()

    def product(z, j):
        at = pl.ds(pl.multiple_of(z * chip_rows, chip_rows), chip_rows)
        return jnp.dot(weights[at, :], amps[j], preferred_element_type=jnp.float32)

    def compute(j):
        own[j].wait()
        pair_wait(j)
        near_wait(2, j)
        for a in range(2):
            pass_copy(a, j).wait_recv()
        other[...] = product(1 - z_lo, j)
        value = other[...]
        most = jnp.maximum(jnp.max(jnp.abs(value), axis=0, keepdims=True), LEAST)
        scales[j] = jnp.broadcast_to(most * (1.0 / TOP), (8, width))
        coded[j] = jnp.round(value * (TOP / most)).astype(jnp.int32).astype(jnp.int16)
        for copy in sum_copy(j):
            copy.start()
        kept[j] = product(z_lo, j)

    def finish(j):
        for copy in sum_copy(j):
            copy.wait_recv()
        scale = scales_in[j, 0:1, :]
        e = energy[0]

        def total(q):
            at = pl.ds(pl.multiple_of(q * rows, rows), rows)
            return (
                kept[j, at, :]
                + coded_in[j, at, :].astype(jnp.int32).astype(jnp.float32) * scale
                + e * amps[j, at, :].astype(jnp.float32)
            )

        stage[j] = total(1 - core)
        end_copy(j).start()
        out[:, columns(core, j)] = total(core)

    forward(0)
    for j in range(CHUNKS):
        if j + 1 < CHUNKS:
            forward(j + 1)
        if j == 0:
            op0_on_in = remote(
                raw.at[0, core], raw.at[0, 1 - core], op_send.at[6], op_recv.at[6], sibling
            )
            op0_on_in.wait_recv()
            mask(0, 5, 1 - core, 1 - z_lo)
        compute(j)
        if j >= 1:
            finish(j - 1)
    finish(CHUNKS - 1)

    for copy in ops + [op0, op0_on]:
        copy.wait_send()
    for j in range(CHUNKS):
        for a in range(3):
            for q in range(2):
                near_copy(a, j, q).wait_send()
        for a in range(2):
            pass_copy(a, j).wait_send()
        pair_copy(j).wait_send()
        for copy in sum_copy(j):
            copy.wait_send()
        end_copy(j).wait_send()
        end_wait(j)


def per_device(psi, h_imp, hops, patterns, signs, bath_energy):
    local = psi[0]
    rows, rest = local.shape
    imps = h_imp.shape[0]
    half = rest // 2
    width = half // CHUNKS
    dma = pltpu.SemaphoreType.DMA
    anywhere = pl.BlockSpec(memory_space=pl.ANY)
    scalar = pl.BlockSpec(memory_space=pltpu.SMEM)
    applied = pl.pallas_call(
        kernel,
        out_shape=jax.ShapeDtypeStruct((rows, rest), jnp.float32),
        in_specs=[anywhere, anywhere, anywhere, scalar, scalar, scalar],
        out_specs=pl.BlockSpec(memory_space=pltpu.VMEM),
        scratch_shapes=[
            pltpu.VMEM((5, 2, imps, rows), jnp.bfloat16),
            pltpu.VMEM((imps, 12 * rows), jnp.bfloat16),
            pltpu.VMEM((CHUNKS, 12 * rows, width), jnp.bfloat16),
            pltpu.VMEM((CHUNKS, 2 * rows, width), jnp.float32),
            pltpu.VMEM((2 * rows, width), jnp.float32),
            pltpu.VMEM((CHUNKS, 2 * rows, width), jnp.int16),
            pltpu.VMEM((CHUNKS, 8, width), jnp.float32),
            pltpu.VMEM((CHUNKS, 2 * rows, width), jnp.int16),
            pltpu.VMEM((CHUNKS, 8, width), jnp.float32),
            pltpu.VMEM((CHUNKS, rows, width), jnp.float32),
            dma((CHUNKS,)),
            dma((5,)),
            dma((3, CHUNKS, 2)),
            dma((3, CHUNKS, 2)),
            dma((CHUNKS,)),
            dma((CHUNKS,)),
            dma((2, CHUNKS)),
            dma((2, CHUNKS)),
            dma((CHUNKS, 2)),
            dma((CHUNKS, 2)),
            dma((CHUNKS,)),
            dma((CHUNKS,)),
            dma((7,)),
            dma((7,)),
        ],
        compiler_params=pltpu.CompilerParams(
            collective_id=0, has_side_effects=True, vmem_limit_bytes=50 * 1024 * 1024
        ),
    )(local, h_imp, hops, patterns, signs, bath_energy)
    return applied[None]


def solution(mesh):
    placed = (
        P("bath", "imp", None),
        P(None, "imp"),
        P(None, None, None, "imp"),
        P(),
        P(None, "bath", None),
        P("bath"),
    )
    return jax.shard_map(
        per_device, mesh=mesh, in_specs=placed, out_specs=P("bath", "imp", None), check_vma=False
    )
```

```python
import jax
import jax.numpy as jnp
from jax import lax
from jax.experimental import pallas as pl
from jax.experimental.pallas import tpu as pltpu
from jax.sharding import PartitionSpec as P

MESH = pl.DeviceIdType.MESH
CHUNKS = 8
LEAST = 1e-30
TOP = 32767.0
AHEAD = 2
BEHIND = 2
BLK = 128


def flip(index, bit):
    return index + bit - 2 * bit * ((index // bit) % 2)


def kernel(
    psi, h_imp, hops, patterns_in, signs_in, energy, out,
    raw, weights, amps, local, kept, stage, coded, scales, coded_in, scales_in, patterns, signs,
    own_sem, mat_sem, small_sem, near_send, near_recv, pair_send, pair_recv, pass_send, pass_recv,
    sum_send, sum_recv, kept_send, kept_recv, op_send, op_recv, zero_send, zero_recv,
):
    bath, imp = lax.axis_index("bath"), lax.axis_index("imp")
    z_lo, core = imp // 2, imp % 2
    side = [(bath // (1 << level)) % 2 for level in range(5)]
    rows, rest = psi.shape
    half = rest // 2
    width = half // CHUNKS
    chip_rows = 2 * rows

    sibling = (bath, flip(imp, 1))
    across = [(bath, (1 - z_lo) * 2 + q) for q in range(2)]
    near = [
        [(flip(bath, 2), z_lo * 2 + q) for q in range(2)],
        [(flip(bath, 8), z_lo * 2 + q) for q in range(2)],
        [(flip(bath, 1), (1 - z_lo) * 2 + q) for q in range(2)],
    ]
    across_same = (bath, flip(imp, 2))
    near_same = (flip(bath, 1), flip(imp, 2))
    onward = [(flip(flip(bath, 2), 4), imp), (flip(flip(bath, 8), 16), imp)]
    near_slot = (1, 3, 5)
    onward_slot = (2, 4)

    def slot_rows(slot, q):
        return pl.ds(pl.multiple_of(slot * chip_rows + q * rows, rows), rows)

    def columns(q, j):
        return pl.ds(pl.multiple_of(q * half + j * width, 128), width)

    def chip(z):
        return pl.ds(pl.multiple_of(z * chip_rows, chip_rows), chip_rows)

    def remote(src, dst, send, recv, device):
        return pltpu.make_async_remote_copy(
            src_ref=src, dst_ref=dst, send_sem=send, recv_sem=recv, device_id=device, device_id_type=MESH
        )

    small = [
        pltpu.make_async_copy(patterns_in, patterns, small_sem.at[0]),
        pltpu.make_async_copy(signs_in, signs, small_sem.at[1]),
    ]
    own = [
        pltpu.make_async_copy(psi.at[:, columns(core, j)], amps.at[j, slot_rows(0, core), :], own_sem.at[j])
        for j in range(CHUNKS)
    ]
    whole = pltpu.make_async_copy(psi, local, small_sem.at[2])
    mats = [pltpu.make_async_copy(h_imp, weights.at[:, slot_rows(0, core)], mat_sem.at[0])]
    for level in range(1, 5):
        mats.append(pltpu.make_async_copy(hops.at[side[level], level], raw.at[level, core], mat_sem.at[level]))
    for copy in small + mats + own + [whole]:
        copy.start()

    barrier = pltpu.get_barrier_semaphore()
    peers = [sibling] + across + near[0] + near[1] + near[2] + onward
    for peer in peers:
        pl.semaphore_signal(barrier, inc=1, device_id=peer, device_id_type=MESH)
    pl.semaphore_wait(barrier, len(peers))

    def near_copy(a, j, q, source):
        return remote(
            psi.at[:, columns(q, j)],
            amps.at[j, slot_rows(near_slot[a], source), :],
            near_send.at[a, j, q],
            near_recv.at[a, j, source],
            near[a][q],
        )

    def near_wait(a, j):
        for q in range(2):
            near_copy(a, j, q, q).wait_recv()

    def pair_copy(j, source):
        return remote(
            psi.at[:, columns(1 - core, j)],
            amps.at[j, slot_rows(0, source), :],
            pair_send.at[j],
            pair_recv.at[j],
            sibling,
        )

    def pass_copy(a, j):
        src = pl.ds(near_slot[a] * chip_rows, chip_rows)
        dst = pl.ds(onward_slot[a] * chip_rows, chip_rows)
        return remote(
            amps.at[j, src, :], amps.at[j, dst, :], pass_send.at[a, j], pass_recv.at[a, j], onward[a]
        )

    def sum_copy(j, q, source):
        return (
            remote(
                coded.at[j, q], coded_in.at[j, source], sum_send.at[j, q, 0], sum_recv.at[j, source, 0], across[q]
            ),
            remote(
                scales.at[j, q], scales_in.at[j, source], sum_send.at[j, q, 1], sum_recv.at[j, source, 1], across[q]
            ),
        )

    def kept_copy(j, source):
        return remote(stage.at[j], kept.at[j, source], kept_send.at[j], kept_recv.at[j], sibling)

    zero = [
        remote(
            hops.at[side[0], 0, chip(z_lo), :], raw.at[0, core, chip(z_lo), :],
            zero_send.at[0], zero_recv.at[0], across_same,
        ),
        remote(
            hops.at[1 - side[0], 0, chip(1 - z_lo), :], raw.at[0, core, chip(1 - z_lo), :],
            zero_send.at[1], zero_recv.at[1], near_same,
        ),
    ]
    zero_in = [
        remote(
            hops.at[side[0], 0, chip(1 - z_lo), :], raw.at[0, core, chip(1 - z_lo), :],
            zero_send.at[0], zero_recv.at[0], across_same,
        ),
        remote(
            hops.at[side[0], 0, chip(z_lo), :], raw.at[0, core, chip(z_lo), :],
            zero_send.at[1], zero_recv.at[1], near_same,
        ),
    ]

    def zero_on(i, source):
        at = chip(1 - z_lo) if i == 0 else chip(z_lo)
        return remote(
            raw.at[0, core, at, :], raw.at[0, source, at, :], zero_send.at[2 + i], zero_recv.at[2 + i], sibling
        )

    ops = [remote(h_imp, weights.at[:, slot_rows(0, core)], op_send.at[0], op_recv.at[0], sibling)]
    for level in range(1, 5):
        ops.append(
            remote(
                hops.at[side[level], level], raw.at[level, core], op_send.at[level], op_recv.at[level], sibling
            )
        )

    zero[0].start()
    zero[1].start()
    for j in range(CHUNKS):
        for q in range(2):
            for a in range(3):
                near_copy(a, j, q, core).start()
        pair_copy(j, core).start()
        if j == 0:
            for copy in ops:
                copy.start()

    def mask(level, slot, q, from_z, first, count):
        def block(p, carry):
            sign = (1 - 2 * signs[level, 0, first + p]).astype(jnp.float32)
            at = pl.ds(pl.multiple_of((first + p) * BLK, BLK), BLK)
            for k in range(rows // BLK):
                keep = patterns[side[level], level, first + p, from_z * 4 + q * 2 + k].astype(jnp.float32)
                factor = jnp.full((BLK, BLK), keep * sign, jnp.float32).astype(jnp.bfloat16)
                to = pl.ds(pl.multiple_of(slot * chip_rows + q * rows + k * BLK, BLK), BLK)
                weights[at, to] = raw[level, q, at, k * BLK : (k + 1) * BLK] * factor
            return carry

        lax.fori_loop(0, count, block, 0)

    def forward(j):
        for a in range(2):
            near_wait(a, j)
            pass_copy(a, j).start()

    def product(z, q, j):
        at = pl.ds(pl.multiple_of(z * chip_rows + q * rows, rows), rows)
        return jnp.dot(weights[at, :], amps[j], preferred_element_type=jnp.float32)

    def compute(j):
        own[j].wait()
        pair_copy(j, core).wait_recv()
        near_wait(2, j)
        for a in range(2):
            pass_copy(a, j).wait_recv()
        for q in range(2):
            value = product(1 - z_lo, q, j)
            most = jnp.maximum(jnp.max(jnp.abs(value), axis=0, keepdims=True), LEAST)
            scales[j, q] = most * (1.0 / TOP)
            coded[j, q] = jnp.round(value * (TOP / most)).astype(jnp.int32).astype(jnp.int16)
            for copy in sum_copy(j, q, core):
                copy.start()
        stage[j] = product(z_lo, 1 - core, j)
        kept_copy(j, core).start()
        kept[j, core] = product(z_lo, core, j)

    def finish(j):
        kept_copy(j, core).wait_recv()
        e = energy[0]
        for q in range(2):
            for copy in sum_copy(j, q, q):
                copy.wait_recv()
            at = slice(q * half + j * width, q * half + (j + 1) * width)
            out[:, at] = (
                kept[j, q]
                + coded_in[j, q].astype(jnp.int32).astype(jnp.float32) * scales_in[j, q]
                + e * local[:, at].astype(jnp.float32)
            )

    for copy in small:
        copy.wait()
    for level in range(1, 5):
        mats[level].wait()
        mask(level, level, core, z_lo, 0, 8)
    forward(0)
    for level in range(1, 5):
        ops[level].wait_recv()
        mask(level, level, 1 - core, z_lo, 0, 8)
    mats[0].wait()
    ops[0].wait_recv()
    whole.wait()
    for j in range(1, AHEAD):
        forward(j)
    for i in range(2):
        zero_in[i].wait_recv()
        zero_on(i, core).start()
        mask(0, 5, core, 1 - z_lo, ((1 - z_lo) if i == 0 else z_lo) * 4, 4)
    for i in range(2):
        zero_on(i, 1 - core).wait_recv()
        mask(0, 5, 1 - core, 1 - z_lo, ((1 - z_lo) if i == 0 else z_lo) * 4, 4)

    for j in range(CHUNKS):
        if j + AHEAD < CHUNKS:
            forward(j + AHEAD)
        compute(j)
        if j >= BEHIND:
            finish(j - BEHIND)
    for j in range(CHUNKS - BEHIND, CHUNKS):
        finish(j)

    for copy in ops + zero + [zero_on(i, core) for i in range(2)]:
        copy.wait_send()
    for j in range(CHUNKS):
        for q in range(2):
            for a in range(3):
                near_copy(a, j, q, core).wait_send()
            for copy in sum_copy(j, q, core):
                copy.wait_send()
        for a in range(2):
            pass_copy(a, j).wait_send()
        pair_copy(j, core).wait_send()
        kept_copy(j, core).wait_send()


def per_device(psi, h_imp, hops, patterns, signs, bath_energy):
    here = psi[0]
    rows, rest = here.shape
    imps = h_imp.shape[0]
    width = rest // 2 // CHUNKS
    n = CHUNKS
    dma = pltpu.SemaphoreType.DMA
    anywhere = pl.BlockSpec(memory_space=pltpu.HBM)
    scalar = pl.BlockSpec(memory_space=pltpu.SMEM)
    operands = [pltpu.with_memory_space_constraint(x, pltpu.HBM) for x in (here, h_imp, hops, patterns, signs)]
    applied = pl.pallas_call(
        kernel,
        out_shape=pltpu.VMEM((rows, rest), jnp.float32),
        in_specs=[anywhere] * 5 + [scalar],
        out_specs=pl.BlockSpec(memory_space=pltpu.VMEM),
        scratch_shapes=[
            pltpu.VMEM((5, 2, imps, rows), jnp.bfloat16),
            pltpu.VMEM((imps, 12 * rows), jnp.bfloat16),
            pltpu.VMEM((n, 12 * rows, width), jnp.bfloat16),
            pltpu.VMEM((rows, rest), jnp.bfloat16),
            pltpu.VMEM((n, 2, rows, width), jnp.float32),
            pltpu.VMEM((n, rows, width), jnp.float32),
            pltpu.VMEM((n, 2, rows, width), jnp.int16),
            pltpu.VMEM((n, 2, 1, width), jnp.float32),
            pltpu.VMEM((n, 2, rows, width), jnp.int16),
            pltpu.VMEM((n, 2, 1, width), jnp.float32),
            pltpu.SMEM(patterns.shape, jnp.int32),
            pltpu.SMEM(signs.shape, jnp.int32),
            dma((n,)), dma((5,)), dma((3,)),
            dma((3, n, 2)), dma((3, n, 2)),
            dma((n,)), dma((n,)),
            dma((2, n)), dma((2, n)),
            dma((n, 2, 2)), dma((n, 2, 2)),
            dma((n,)), dma((n,)),
            dma((5,)), dma((5,)),
            dma((4,)), dma((4,)),
        ],
        compiler_params=pltpu.CompilerParams(
            collective_id=0, has_side_effects=True, vmem_limit_bytes=50 * 1024 * 1024
        ),
    )(*operands, bath_energy)
    return applied[None]


def solution(mesh):
    placed = (
        P("bath", "imp", None),
        P(None, "imp"),
        P(None, None, None, "imp"),
        P(),
        P(None, "bath", None),
        P("bath"),
    )
    return jax.shard_map(
        per_device, mesh=mesh, in_specs=placed, out_specs=P("bath", "imp", None), check_vma=False
    )
```

```python
import jax
import jax.numpy as jnp
from jax import lax
from jax.experimental import pallas as pl
from jax.experimental.pallas import tpu as pltpu
from jax.sharding import PartitionSpec as P

MESH = pl.DeviceIdType.MESH
CHUNKS = 8
LEAST = 1e-30
TOP = 32767.0
AHEAD = 2
BEHIND = 3
LATE = 3
LEFT = 128
BLK = 128


def flip(index, bit):
    return index + bit - 2 * bit * ((index // bit) % 2)


def kernel(
    psi, h_imp, hops, patterns_in, signs_in, energy, out,
    raw, weights, amps, local, kept, stage, coded, scales, coded_in, scales_in, early, patterns, signs,
    own_sem, mat_sem, small_sem, near_send, near_recv, pair_send, pair_recv, pass_send, pass_recv,
    sum_send, sum_recv, kept_send, kept_recv, op_send, op_recv, zero_send, zero_recv, early_send, early_recv,
):
    bath, imp = lax.axis_index("bath"), lax.axis_index("imp")
    z_lo, core = imp // 2, imp % 2
    side = [(bath // (1 << level)) % 2 for level in range(5)]
    rows, rest = psi.shape
    half = rest // 2
    width = half // CHUNKS
    chip_rows = 2 * rows

    sibling = (bath, flip(imp, 1))
    across = [(bath, (1 - z_lo) * 2 + q) for q in range(2)]
    near = [
        [(flip(bath, 2), z_lo * 2 + q) for q in range(2)],
        [(flip(bath, 8), z_lo * 2 + q) for q in range(2)],
        [(flip(bath, 1), (1 - z_lo) * 2 + q) for q in range(2)],
    ]
    across_same = (bath, flip(imp, 2))
    near_same = (flip(bath, 1), flip(imp, 2))
    onward = [(flip(flip(bath, 2), 4), imp), (flip(flip(bath, 8), 16), imp)]
    onward_both = [[(to[0], z_lo * 2 + q) for q in range(2)] for to in onward]
    near_as_onward = [(flip(bath, 2), imp), (flip(bath, 8), imp)]
    near_slot = (1, 3, 5)
    onward_slot = (2, 4)

    def slot_rows(slot, q):
        return pl.ds(pl.multiple_of(slot * chip_rows + q * rows, rows), rows)

    def columns(q, j):
        return pl.ds(pl.multiple_of(q * half + j * width, 128), width)

    def chip(z):
        return pl.ds(pl.multiple_of(z * chip_rows, chip_rows), chip_rows)

    def remote(src, dst, send, recv, device):
        return pltpu.make_async_remote_copy(
            src_ref=src, dst_ref=dst, send_sem=send, recv_sem=recv, device_id=device, device_id_type=MESH
        )

    small = [
        pltpu.make_async_copy(patterns_in, patterns, small_sem.at[0]),
        pltpu.make_async_copy(signs_in, signs, small_sem.at[1]),
    ]

    def own_copy(j):
        return pltpu.make_async_copy(psi.at[:, columns(core, j)], amps.at[j, slot_rows(0, core), :], own_sem.at[j])

    whole = pltpu.make_async_copy(psi, local, small_sem.at[2])
    mats = [pltpu.make_async_copy(h_imp, weights.at[:, slot_rows(0, core)], mat_sem.at[0])]
    for level in range(1, 5):
        mats.append(pltpu.make_async_copy(hops.at[side[level], level], raw.at[level, core], mat_sem.at[level]))
    for copy in small + mats + [whole]:
        copy.start()

    @pl.loop(0, CHUNKS)
    def _(j):
        own_copy(j).start()

    barrier = pltpu.get_barrier_semaphore()
    peers = [sibling] + across + near[0] + near[1] + near[2] + onward_both[0] + onward_both[1]
    for peer in peers:
        pl.semaphore_signal(barrier, inc=1, device_id=peer, device_id_type=MESH)
    pl.semaphore_wait(barrier, len(peers))

    def near_copy(a, j, q, source):
        return remote(
            psi.at[:, columns(q, j)],
            amps.at[j, slot_rows(near_slot[a], source), :],
            near_send.at[a, j, q],
            near_recv.at[a, j, source],
            near[a][q],
        )

    def near_wait(a, j):
        for q in range(2):
            near_copy(a, j, q, q).wait_recv()

    def pair_copy(j, source):
        return remote(
            psi.at[:, columns(1 - core, j)],
            amps.at[j, slot_rows(0, source), :],
            pair_send.at[j],
            pair_recv.at[j],
            sibling,
        )

    def pass_copy(a, j):
        src = pl.ds(near_slot[a] * chip_rows, chip_rows)
        dst = pl.ds(onward_slot[a] * chip_rows, chip_rows)
        return remote(
            amps.at[j, src, :], amps.at[j, dst, :], pass_send.at[a, j], pass_recv.at[a, j], onward[a]
        )

    def sum_copy(j, q, source):
        return (
            remote(
                coded.at[j, q], coded_in.at[j, source], sum_send.at[j, q, 0], sum_recv.at[j, source, 0], across[q]
            ),
            remote(
                scales.at[j, q], scales_in.at[j, source], sum_send.at[j, q, 1], sum_recv.at[j, source, 1], across[q]
            ),
        )

    def kept_copy(j, source):
        return remote(stage.at[j], kept.at[j, source], kept_send.at[j], kept_recv.at[j], sibling)

    def early_copy(a, q, source):
        return remote(
            psi.at[:, columns(q, CHUNKS - 1)],
            early.at[a, pl.ds(pl.multiple_of(source * rows, rows), rows), :],
            early_send.at[a, q],
            early_recv.at[a, source],
            onward_both[a][q],
        )

    def early_pass(a):
        dst = pl.ds(onward_slot[a] * chip_rows, chip_rows)
        return remote(
            early.at[a],
            amps.at[CHUNKS - 1, dst, :],
            pass_send.at[a, CHUNKS - 1],
            pass_recv.at[a, CHUNKS - 1],
            near_as_onward[a],
        )

    pieces = ((1, 0, chip_rows), (0, 0, LEFT), (0, LEFT, chip_rows - LEFT))

    def piece(i, z):
        swap, first, count = pieces[i]
        owner = 1 - z if swap else z
        return owner * chip_rows + first, count

    def zero_copy(i):
        first, count = piece(i, 1 - z_lo)
        at = pl.ds(pl.multiple_of(first, BLK), count)
        far = i == 2
        return remote(
            hops.at[(1 - side[0]) if far else side[0], 0, at, :], raw.at[0, core, at, :],
            zero_send.at[i], zero_recv.at[i], near_same if far else across_same,
        )

    def zero_in(i):
        first, count = piece(i, z_lo)
        at = pl.ds(pl.multiple_of(first, BLK), count)
        return remote(
            hops.at[side[0], 0, at, :], raw.at[0, core, at, :],
            zero_send.at[i], zero_recv.at[i], near_same if i == 2 else across_same,
        )

    def zero_on(i, source):
        first, count = piece(i, z_lo)
        at = pl.ds(pl.multiple_of(first, BLK), count)
        return remote(
            raw.at[0, source, at, :], raw.at[0, source, at, :], zero_send.at[3 + i], zero_recv.at[3 + i], sibling
        )

    def zero_take(i):
        zero_in(i).wait_recv()
        zero_on(i, core).start()
        first, count = piece(i, z_lo)
        mask(0, 5, core, 1 - z_lo, first // BLK, count // BLK)

    def zero_rest(i):
        zero_on(i, 1 - core).wait_recv()
        first, count = piece(i, z_lo)
        mask(0, 5, 1 - core, 1 - z_lo, first // BLK, count // BLK)

    ops = [remote(h_imp, weights.at[:, slot_rows(0, core)], op_send.at[0], op_recv.at[0], sibling)]
    for level in range(1, 5):
        ops.append(
            remote(
                hops.at[side[level], level], raw.at[level, core], op_send.at[level], op_recv.at[level], sibling
            )
        )

    zero_copy(0).start()
    zero_copy(1).start()

    def send(j):
        for q in range(2):
            for a in range(3):
                near_copy(a, j, q, core).start()
        pair_copy(j, core).start()

    send(0)
    zero_copy(2).start()
    for a in range(2):
        for q in range(2):
            early_copy(a, q, core).start()
    for copy in ops:
        copy.start()
    pl.loop(1, CHUNKS)(send)

    def mask(level, slot, q, from_z, first, count):
        def block(p, carry):
            sign = (1 - 2 * signs[level, 0, first + p]).astype(jnp.float32)
            at = pl.ds(pl.multiple_of((first + p) * BLK, BLK), BLK)
            for k in range(rows // BLK):
                keep = patterns[side[level], level, first + p, from_z * 4 + q * 2 + k].astype(jnp.float32)
                factor = jnp.full((BLK, BLK), keep * sign, jnp.float32).astype(jnp.bfloat16)
                to = pl.ds(pl.multiple_of(slot * chip_rows + q * rows + k * BLK, BLK), BLK)
                weights[at, to] = raw[level, q, at, k * BLK : (k + 1) * BLK] * factor
            return carry

        lax.fori_loop(0, count, block, 0)

    def forward(j):
        for a in range(2):
            near_wait(a, j)
            pass_copy(a, j).start()

    def product(z, q, j):
        at = pl.ds(pl.multiple_of(z * chip_rows + q * rows, rows), rows)
        return jnp.dot(weights[at, :], amps[j], preferred_element_type=jnp.float32)

    def compute(j):
        own_copy(j).wait()
        pair_copy(j, core).wait_recv()
        near_wait(2, j)

        @pl.when(j == CHUNKS - 1)
        def _():
            for a in range(2):
                near_wait(a, j)

        for a in range(2):
            pass_copy(a, j).wait_recv()
        for q in range(2):
            value = product(1 - z_lo, q, j)
            most = jnp.maximum(jnp.max(jnp.abs(value), axis=0, keepdims=True), LEAST)
            scales[j, q] = most * (1.0 / TOP)
            coded[j, q] = jnp.round(value * (TOP / most)).astype(jnp.int32).astype(jnp.int16)
            for copy in sum_copy(j, q, core):
                copy.start()

    def compute_own(j):
        stage[j] = product(z_lo, 1 - core, j)
        kept_copy(j, core).start()
        kept[j, core] = product(z_lo, core, j)

    def finish(j):
        kept_copy(j, core).wait_recv()
        e = energy[0]
        for q in range(2):
            for copy in sum_copy(j, q, q):
                copy.wait_recv()
            at = columns(q, j)
            out[:, at] = (
                kept[j, q]
                + coded_in[j, q].astype(jnp.int32).astype(jnp.float32) * scales_in[j, q]
                + e * local[:, at].astype(jnp.float32)
            )

    for copy in small:
        copy.wait()
    for level in range(1, 5):
        mats[level].wait()
        mask(level, level, core, z_lo, 0, 8)
    forward(0)
    for level in range(1, 5):
        ops[level].wait_recv()
        mask(level, level, 1 - core, z_lo, 0, 8)
    mats[0].wait()
    ops[0].wait_recv()
    whole.wait()
    for j in range(1, AHEAD):
        forward(j)
    zero_take(0)
    for a in range(2):
        for q in range(2):
            early_copy(a, q, q).wait_recv()
        early_pass(a).start()
    zero_rest(0)

    @pl.loop(0, CHUNKS)
    def _(step):
        @pl.when(step + AHEAD < CHUNKS - 1)
        def _():
            forward(step + AHEAD)

        compute(step)

        @pl.when(step == 0)
        def _():
            zero_take(1)
            zero_take(2)

        @pl.when(step == 1)
        def _():
            zero_rest(1)
            zero_rest(2)

        @pl.when((step >= 1) & (step <= CHUNKS - LATE))
        def _():
            compute_own(step - 1)

        @pl.when(step >= BEHIND)
        def _():
            finish(step - BEHIND)

    pl.loop(CHUNKS - LATE, CHUNKS)(compute_own)
    pl.loop(CHUNKS - BEHIND, CHUNKS)(finish)

    for copy in ops:
        copy.wait_send()
    for i in range(3):
        zero_copy(i).wait_send()
        zero_on(i, core).wait_send()
    for a in range(2):
        for q in range(2):
            early_copy(a, q, core).wait_send()

    @pl.loop(0, CHUNKS)
    def _(j):
        for q in range(2):
            for a in range(3):
                near_copy(a, j, q, core).wait_send()
            for copy in sum_copy(j, q, core):
                copy.wait_send()
        for a in range(2):
            pass_copy(a, j).wait_send()
        pair_copy(j, core).wait_send()
        kept_copy(j, core).wait_send()


def per_device(psi, h_imp, hops, patterns, signs, bath_energy):
    here = psi[0]
    rows, rest = here.shape
    imps = h_imp.shape[0]
    width = rest // 2 // CHUNKS
    n = CHUNKS
    dma = pltpu.SemaphoreType.DMA
    anywhere = pl.BlockSpec(memory_space=pltpu.HBM)
    scalar = pl.BlockSpec(memory_space=pltpu.SMEM)
    operands = [pltpu.with_memory_space_constraint(x, pltpu.HBM) for x in (here, h_imp, hops, patterns, signs)]
    applied = pl.pallas_call(
        kernel,
        out_shape=pltpu.VMEM((rows, rest), jnp.float32),
        in_specs=[anywhere] * 5 + [scalar],
        out_specs=pl.BlockSpec(memory_space=pltpu.VMEM),
        scratch_shapes=[
            pltpu.VMEM((5, 2, imps, rows), jnp.bfloat16),
            pltpu.VMEM((imps, 12 * rows), jnp.bfloat16),
            pltpu.VMEM((n, 12 * rows, width), jnp.bfloat16),
            pltpu.VMEM((rows, rest), jnp.bfloat16),
            pltpu.VMEM((n, 2, rows, width), jnp.float32),
            pltpu.VMEM((n, rows, width), jnp.float32),
            pltpu.VMEM((n, 2, rows, width), jnp.int16),
            pltpu.VMEM((n, 2, 1, width), jnp.float32),
            pltpu.VMEM((n, 2, rows, width), jnp.int16),
            pltpu.VMEM((n, 2, 1, width), jnp.float32),
            pltpu.VMEM((2, 2 * rows, width), jnp.bfloat16),
            pltpu.SMEM(patterns.shape, jnp.int32),
            pltpu.SMEM(signs.shape, jnp.int32),
            dma((n,)), dma((5,)), dma((3,)),
            dma((3, n, 2)), dma((3, n, 2)),
            dma((n,)), dma((n,)),
            dma((2, n)), dma((2, n)),
            dma((n, 2, 2)), dma((n, 2, 2)),
            dma((n,)), dma((n,)),
            dma((5,)), dma((5,)),
            dma((6,)), dma((6,)),
            dma((2, 2)), dma((2, 2)),
        ],
        compiler_params=pltpu.CompilerParams(
            collective_id=0, has_side_effects=True, vmem_limit_bytes=50 * 1024 * 1024
        ),
    )(*operands, bath_energy)
    return applied[None]


def solution(mesh):
    placed = (
        P("bath", "imp", None),
        P(None, "imp"),
        P(None, None, None, "imp"),
        P(),
        P(None, "bath", None),
        P("bath"),
    )
    return jax.shard_map(
        per_device, mesh=mesh, in_specs=placed, out_specs=P("bath", "imp", None), check_vma=False
    )
```

```python
import jax
import jax.numpy as jnp
from jax import lax
from jax.experimental import pallas as pl
from jax.experimental.pallas import tpu as pltpu
from jax.sharding import PartitionSpec as P

MESH = pl.DeviceIdType.MESH
CHUNKS = 8
LEAST = 1e-30
TOP = 32767.0
AHEAD = 2
BEHIND = 4
LATE = 3
LEFT = 128
BLK = 128


def flip(index, bit):
    return index + bit - 2 * bit * ((index // bit) % 2)


def kernel(
    psi, h_imp, hops, patterns_in, signs_in, energy, out,
    raw, weights, amps, local, kept, stage, coded, scales, coded_in, scales_in, early, patterns, signs,
    own_sem, mat_sem, small_sem, near_send, near_recv, pair_send, pair_recv, pass_send, pass_recv,
    sum_send, sum_recv, kept_send, kept_recv, op_send, op_recv, zero_send, zero_recv, early_send, early_recv,
):
    bath, imp = lax.axis_index("bath"), lax.axis_index("imp")
    z_lo, core = imp // 2, imp % 2
    side = [(bath // (1 << level)) % 2 for level in range(5)]
    rows, rest = psi.shape
    half = rest // 2
    width = half // CHUNKS
    chip_rows = 2 * rows

    sibling = (bath, flip(imp, 1))
    across = [(bath, (1 - z_lo) * 2 + q) for q in range(2)]
    near = [
        [(flip(bath, 2), z_lo * 2 + q) for q in range(2)],
        [(flip(bath, 8), z_lo * 2 + q) for q in range(2)],
        [(flip(bath, 1), (1 - z_lo) * 2 + q) for q in range(2)],
    ]
    across_same = (bath, flip(imp, 2))
    near_same = (flip(bath, 1), flip(imp, 2))
    onward = [(flip(flip(bath, 2), 4), imp), (flip(flip(bath, 8), 16), imp)]
    onward_both = [[(to[0], z_lo * 2 + q) for q in range(2)] for to in onward]
    near_as_onward = [(flip(bath, 2), imp), (flip(bath, 8), imp)]
    near_slot = (1, 3, 5)
    onward_slot = (2, 4)

    def slot_rows(slot, q):
        return pl.ds(pl.multiple_of(slot * chip_rows + q * rows, rows), rows)

    def columns(q, j):
        return pl.ds(pl.multiple_of(q * half + j * width, 128), width)

    def chip(z):
        return pl.ds(pl.multiple_of(z * chip_rows, chip_rows), chip_rows)

    def remote(src, dst, send, recv, device):
        return pltpu.make_async_remote_copy(
            src_ref=src, dst_ref=dst, send_sem=send, recv_sem=recv, device_id=device, device_id_type=MESH
        )

    small = [
        pltpu.make_async_copy(patterns_in, patterns, small_sem.at[0]),
        pltpu.make_async_copy(signs_in, signs, small_sem.at[1]),
    ]

    def own_copy(j):
        return pltpu.make_async_copy(psi.at[:, columns(core, j)], amps.at[j, slot_rows(0, core), :], own_sem.at[j])

    whole = pltpu.make_async_copy(psi, local, small_sem.at[2])
    mats = [pltpu.make_async_copy(h_imp, weights.at[:, slot_rows(0, core)], mat_sem.at[0])]
    for level in range(1, 5):
        mats.append(pltpu.make_async_copy(hops.at[side[level], level], raw.at[level, core], mat_sem.at[level]))
    barrier = pltpu.get_barrier_semaphore()
    peers = [sibling] + across + near[0] + near[1] + near[2] + onward_both[0] + onward_both[1]
    for peer in peers:
        pl.semaphore_signal(barrier, inc=1, device_id=peer, device_id_type=MESH)
    for copy in [whole] + small + mats:
        copy.start()

    @pl.loop(0, CHUNKS)
    def _(j):
        own_copy(j).start()

    whole.wait()
    pl.semaphore_wait(barrier, len(peers))

    def near_copy(a, j, q, source):
        return remote(
            local.at[:, columns(q, j)],
            amps.at[j, slot_rows(near_slot[a], source), :],
            near_send.at[a, j, q],
            near_recv.at[a, j, source],
            near[a][q],
        )

    def near_wait(a, j):
        for q in range(2):
            near_copy(a, j, q, q).wait_recv()

    def pair_copy(j, source):
        return remote(
            local.at[:, columns(1 - core, j)],
            amps.at[j, slot_rows(0, source), :],
            pair_send.at[j],
            pair_recv.at[j],
            sibling,
        )

    def pass_copy(a, j):
        src = pl.ds(near_slot[a] * chip_rows, chip_rows)
        dst = pl.ds(onward_slot[a] * chip_rows, chip_rows)
        return remote(
            amps.at[j, src, :], amps.at[j, dst, :], pass_send.at[a, j], pass_recv.at[a, j], onward[a]
        )

    def sum_copy(j, q, source):
        return (
            remote(
                coded.at[j, q], coded_in.at[j, source], sum_send.at[j, q, 0], sum_recv.at[j, source, 0], across[q]
            ),
            remote(
                scales.at[j, q], scales_in.at[j, source], sum_send.at[j, q, 1], sum_recv.at[j, source, 1], across[q]
            ),
        )

    def kept_copy(j, source):
        return remote(stage.at[j], kept.at[j, source], kept_send.at[j], kept_recv.at[j], sibling)

    def early_copy(a, q, source):
        return remote(
            local.at[:, columns(q, CHUNKS - 1)],
            early.at[a, pl.ds(pl.multiple_of(source * rows, rows), rows), :],
            early_send.at[a, q],
            early_recv.at[a, source],
            onward_both[a][q],
        )

    def early_pass(a):
        dst = pl.ds(onward_slot[a] * chip_rows, chip_rows)
        return remote(
            early.at[a],
            amps.at[CHUNKS - 1, dst, :],
            pass_send.at[a, CHUNKS - 1],
            pass_recv.at[a, CHUNKS - 1],
            near_as_onward[a],
        )

    pieces = ((1, 0, chip_rows), (0, 0, LEFT), (0, LEFT, chip_rows - LEFT))

    def piece(i, z):
        swap, first, count = pieces[i]
        owner = 1 - z if swap else z
        return owner * chip_rows + first, count

    def zero_copy(i):
        first, count = piece(i, 1 - z_lo)
        at = pl.ds(pl.multiple_of(first, BLK), count)
        far = i == 2
        return remote(
            hops.at[(1 - side[0]) if far else side[0], 0, at, :], raw.at[0, core, at, :],
            zero_send.at[i], zero_recv.at[i], near_same if far else across_same,
        )

    def zero_in(i):
        first, count = piece(i, z_lo)
        at = pl.ds(pl.multiple_of(first, BLK), count)
        return remote(
            hops.at[side[0], 0, at, :], raw.at[0, core, at, :],
            zero_send.at[i], zero_recv.at[i], near_same if i == 2 else across_same,
        )

    def zero_on(i, source):
        first, count = piece(i, z_lo)
        at = pl.ds(pl.multiple_of(first, BLK), count)
        return remote(
            raw.at[0, source, at, :], raw.at[0, source, at, :], zero_send.at[3 + i], zero_recv.at[3 + i], sibling
        )

    def zero_take(i):
        zero_in(i).wait_recv()
        zero_on(i, core).start()
        first, count = piece(i, z_lo)
        mask(0, 5, core, 1 - z_lo, first // BLK, count // BLK)

    def zero_rest(i):
        zero_on(i, 1 - core).wait_recv()
        first, count = piece(i, z_lo)
        mask(0, 5, 1 - core, 1 - z_lo, first // BLK, count // BLK)

    ops = [remote(h_imp, weights.at[:, slot_rows(0, core)], op_send.at[0], op_recv.at[0], sibling)]
    for level in range(1, 5):
        ops.append(
            remote(
                hops.at[side[level], level], raw.at[level, core], op_send.at[level], op_recv.at[level], sibling
            )
        )

    zero_copy(0).start()
    zero_copy(1).start()

    def send(j):
        for q in range(2):
            for a in range(3):
                near_copy(a, j, q, core).start()
        pair_copy(j, core).start()

    send(0)
    zero_copy(2).start()
    for a in range(2):
        for q in range(2):
            early_copy(a, q, core).start()
    for copy in ops:
        copy.start()
    pl.loop(1, CHUNKS)(send)

    def mask(level, slot, q, from_z, first, count):
        def block(p, carry):
            sign = (1 - 2 * signs[level, 0, first + p]).astype(jnp.float32)
            at = pl.ds(pl.multiple_of((first + p) * BLK, BLK), BLK)
            for k in range(rows // BLK):
                keep = patterns[side[level], level, first + p, from_z * 4 + q * 2 + k].astype(jnp.float32)
                factor = jnp.full((BLK, BLK), keep * sign, jnp.float32).astype(jnp.bfloat16)
                to = pl.ds(pl.multiple_of(slot * chip_rows + q * rows + k * BLK, BLK), BLK)
                weights[at, to] = raw[level, q, at, k * BLK : (k + 1) * BLK] * factor
            return carry

        lax.fori_loop(0, count, block, 0)

    def forward(j):
        for a in range(2):
            near_wait(a, j)
            pass_copy(a, j).start()

    def product(z, q, j):
        at = pl.ds(pl.multiple_of(z * chip_rows + q * rows, rows), rows)
        return jnp.dot(weights[at, :], amps[j], preferred_element_type=jnp.float32)

    def compute(j):
        own_copy(j).wait()
        pair_copy(j, core).wait_recv()
        near_wait(2, j)

        @pl.when(j == CHUNKS - 1)
        def _():
            for a in range(2):
                near_wait(a, j)

        for a in range(2):
            pass_copy(a, j).wait_recv()
        for q in range(2):
            value = product(1 - z_lo, q, j)
            most = jnp.maximum(jnp.max(jnp.abs(value), axis=0, keepdims=True), LEAST)
            scales[j, q] = most * (1.0 / TOP)
            coded[j, q] = jnp.round(value * (TOP / most)).astype(jnp.int32).astype(jnp.int16)
            for copy in sum_copy(j, q, core):
                copy.start()

    def compute_own(j):
        stage[j] = product(z_lo, 1 - core, j)
        kept_copy(j, core).start()
        kept[j, core] = product(z_lo, core, j)

    def finish(j):
        kept_copy(j, core).wait_recv()
        e = energy[0]
        for q in range(2):
            for copy in sum_copy(j, q, q):
                copy.wait_recv()
            at = columns(q, j)
            out[:, at] = (
                kept[j, q]
                + coded_in[j, q].astype(jnp.int32).astype(jnp.float32) * scales_in[j, q]
                + e * local[:, at].astype(jnp.float32)
            )

    for copy in small:
        copy.wait()
    for level in range(1, 5):
        mats[level].wait()
        mask(level, level, core, z_lo, 0, 8)
    forward(0)
    for level in range(1, 5):
        ops[level].wait_recv()
        mask(level, level, 1 - core, z_lo, 0, 8)
    mats[0].wait()
    ops[0].wait_recv()
    for j in range(1, AHEAD):
        forward(j)
    zero_take(0)
    for a in range(2):
        for q in range(2):
            early_copy(a, q, q).wait_recv()
        early_pass(a).start()
    zero_rest(0)

    @pl.loop(0, CHUNKS)
    def _(step):
        @pl.when(step + AHEAD < CHUNKS - 1)
        def _():
            forward(step + AHEAD)

        @pl.when(step >= BEHIND)
        def _():
            finish(step - BEHIND)

        compute(step)

        @pl.when(step == 0)
        def _():
            zero_take(1)
            zero_take(2)

        @pl.when(step == 1)
        def _():
            zero_rest(1)
            zero_rest(2)

        @pl.when((step >= 1) & (step <= CHUNKS - LATE))
        def _():
            compute_own(step - 1)


    pl.loop(CHUNKS - LATE, CHUNKS)(compute_own)
    pl.loop(CHUNKS - BEHIND, CHUNKS)(finish)

    for copy in ops:
        copy.wait_send()
    for i in range(3):
        zero_copy(i).wait_send()
        zero_on(i, core).wait_send()
    for a in range(2):
        for q in range(2):
            early_copy(a, q, core).wait_send()

    @pl.loop(0, CHUNKS)
    def _(j):
        for q in range(2):
            for a in range(3):
                near_copy(a, j, q, core).wait_send()
            for copy in sum_copy(j, q, core):
                copy.wait_send()
        for a in range(2):
            pass_copy(a, j).wait_send()
        pair_copy(j, core).wait_send()
        kept_copy(j, core).wait_send()


def per_device(psi, h_imp, hops, patterns, signs, bath_energy):
    here = psi[0]
    rows, rest = here.shape
    imps = h_imp.shape[0]
    width = rest // 2 // CHUNKS
    n = CHUNKS
    dma = pltpu.SemaphoreType.DMA
    anywhere = pl.BlockSpec(memory_space=pltpu.HBM)
    scalar = pl.BlockSpec(memory_space=pltpu.SMEM)
    operands = [pltpu.with_memory_space_constraint(x, pltpu.HBM) for x in (here, h_imp, hops, patterns, signs)]
    applied = pl.pallas_call(
        kernel,
        out_shape=pltpu.VMEM((rows, rest), jnp.float32),
        in_specs=[anywhere] * 5 + [scalar],
        out_specs=pl.BlockSpec(memory_space=pltpu.VMEM),
        scratch_shapes=[
            pltpu.VMEM((5, 2, imps, rows), jnp.bfloat16),
            pltpu.VMEM((imps, 12 * rows), jnp.bfloat16),
            pltpu.VMEM((n, 12 * rows, width), jnp.bfloat16),
            pltpu.VMEM((rows, rest), jnp.bfloat16),
            pltpu.VMEM((n, 2, rows, width), jnp.float32),
            pltpu.VMEM((n, rows, width), jnp.float32),
            pltpu.VMEM((n, 2, rows, width), jnp.int16),
            pltpu.VMEM((n, 2, 1, width), jnp.float32),
            pltpu.VMEM((n, 2, rows, width), jnp.int16),
            pltpu.VMEM((n, 2, 1, width), jnp.float32),
            pltpu.VMEM((2, 2 * rows, width), jnp.bfloat16),
            pltpu.SMEM(patterns.shape, jnp.int32),
            pltpu.SMEM(signs.shape, jnp.int32),
            dma((n,)), dma((5,)), dma((3,)),
            dma((3, n, 2)), dma((3, n, 2)),
            dma((n,)), dma((n,)),
            dma((2, n)), dma((2, n)),
            dma((n, 2, 2)), dma((n, 2, 2)),
            dma((n,)), dma((n,)),
            dma((5,)), dma((5,)),
            dma((6,)), dma((6,)),
            dma((2, 2)), dma((2, 2)),
        ],
        compiler_params=pltpu.CompilerParams(
            collective_id=0, has_side_effects=True, vmem_limit_bytes=50 * 1024 * 1024
        ),
    )(*operands, bath_energy)
    return applied[None]


def solution(mesh):
    placed = (
        P("bath", "imp", None),
        P(None, "imp"),
        P(None, None, None, "imp"),
        P(),
        P(None, "bath", None),
        P("bath"),
    )
    return jax.shard_map(
        per_device, mesh=mesh, in_specs=placed, out_specs=P("bath", "imp", None), check_vma=False
    )
```

```python
import jax
import jax.numpy as jnp
from jax import lax
from jax.experimental import pallas as pl
from jax.experimental.pallas import tpu as pltpu
from jax.sharding import PartitionSpec as P

MESH = pl.DeviceIdType.MESH
CHUNKS = 8
LEAST = 1e-30
TOP = 32767.0
AHEAD = 2
BEHIND = 4
LATE = 3
LEFT = 256
BLK = 128


def flip(index, bit):
    return index + bit - 2 * bit * ((index // bit) % 2)


def kernel(
    psi, h_imp, hops, patterns_in, signs_in, energy, out,
    raw, weights, amps, local, kept, stage, coded, scales, coded_in, scales_in, early, patterns, signs,
    own_sem, mat_sem, small_sem, near_send, near_recv, pair_send, pair_recv, pass_send, pass_recv,
    sum_send, sum_recv, kept_send, kept_recv, op_send, op_recv, zero_send, zero_recv, early_send, early_recv,
):
    bath, imp = lax.axis_index("bath"), lax.axis_index("imp")
    z_lo, core = imp // 2, imp % 2
    side = [(bath // (1 << level)) % 2 for level in range(5)]
    rows, rest = psi.shape
    half = rest // 2
    width = half // CHUNKS
    chip_rows = 2 * rows

    sibling = (bath, flip(imp, 1))
    across = [(bath, (1 - z_lo) * 2 + q) for q in range(2)]
    near = [
        [(flip(bath, 2), z_lo * 2 + q) for q in range(2)],
        [(flip(bath, 8), z_lo * 2 + q) for q in range(2)],
        [(flip(bath, 1), (1 - z_lo) * 2 + q) for q in range(2)],
    ]
    across_same = (bath, flip(imp, 2))
    near_same = (flip(bath, 1), flip(imp, 2))
    onward = [(flip(flip(bath, 2), 4), imp), (flip(flip(bath, 8), 16), imp)]
    onward_both = [[(to[0], z_lo * 2 + q) for q in range(2)] for to in onward]
    near_as_onward = [(flip(bath, 2), imp), (flip(bath, 8), imp)]
    near_slot = (1, 3, 5)
    onward_slot = (2, 4)

    def slot_rows(slot, q):
        return pl.ds(pl.multiple_of(slot * chip_rows + q * rows, rows), rows)

    def columns(q, j):
        return pl.ds(pl.multiple_of(q * half + j * width, 128), width)

    def chip(z):
        return pl.ds(pl.multiple_of(z * chip_rows, chip_rows), chip_rows)

    def remote(src, dst, send, recv, device):
        return pltpu.make_async_remote_copy(
            src_ref=src, dst_ref=dst, send_sem=send, recv_sem=recv, device_id=device, device_id_type=MESH
        )

    small = [
        pltpu.make_async_copy(patterns_in, patterns, small_sem.at[0]),
        pltpu.make_async_copy(signs_in, signs, small_sem.at[1]),
    ]

    def own_copy(j):
        return pltpu.make_async_copy(psi.at[:, columns(core, j)], amps.at[j, slot_rows(0, core), :], own_sem.at[j])

    whole = pltpu.make_async_copy(psi, local, small_sem.at[2])
    mats = [pltpu.make_async_copy(h_imp, weights.at[:, slot_rows(0, core)], mat_sem.at[0])]
    for level in range(1, 5):
        mats.append(pltpu.make_async_copy(hops.at[side[level], level], raw.at[level, core], mat_sem.at[level]))
    barrier = pltpu.get_barrier_semaphore()
    peers = [sibling] + across + near[0] + near[1] + near[2] + onward_both[0] + onward_both[1]
    for peer in peers:
        pl.semaphore_signal(barrier, inc=1, device_id=peer, device_id_type=MESH)
    for copy in [whole] + small + mats:
        copy.start()

    @pl.loop(0, CHUNKS)
    def _(j):
        own_copy(j).start()

    whole.wait()
    pl.semaphore_wait(barrier, len(peers))

    def near_copy(a, j, q, source):
        return remote(
            local.at[:, columns(q, j)],
            amps.at[j, slot_rows(near_slot[a], source), :],
            near_send.at[a, j, q],
            near_recv.at[a, j, source],
            near[a][q],
        )

    def near_wait(a, j):
        for q in range(2):
            near_copy(a, j, q, q).wait_recv()

    def pair_copy(j, source):
        return remote(
            local.at[:, columns(1 - core, j)],
            amps.at[j, slot_rows(0, source), :],
            pair_send.at[j],
            pair_recv.at[j],
            sibling,
        )

    def pass_copy(a, j):
        src = pl.ds(near_slot[a] * chip_rows, chip_rows)
        dst = pl.ds(onward_slot[a] * chip_rows, chip_rows)
        return remote(
            amps.at[j, src, :], amps.at[j, dst, :], pass_send.at[a, j], pass_recv.at[a, j], onward[a]
        )

    def sum_copy(j, q, source):
        return (
            remote(
                coded.at[j, q], coded_in.at[j, source], sum_send.at[j, q, 0], sum_recv.at[j, source, 0], across[q]
            ),
            remote(
                scales.at[j, q], scales_in.at[j, source], sum_send.at[j, q, 1], sum_recv.at[j, source, 1], across[q]
            ),
        )

    def kept_copy(j, source):
        return remote(stage.at[j], kept.at[j, source], kept_send.at[j], kept_recv.at[j], sibling)

    def early_copy(a, q, source):
        return remote(
            local.at[:, columns(q, CHUNKS - 1)],
            early.at[a, pl.ds(pl.multiple_of(source * rows, rows), rows), :],
            early_send.at[a, q],
            early_recv.at[a, source],
            onward_both[a][q],
        )

    def early_pass(a):
        dst = pl.ds(onward_slot[a] * chip_rows, chip_rows)
        return remote(
            early.at[a],
            amps.at[CHUNKS - 1, dst, :],
            pass_send.at[a, CHUNKS - 1],
            pass_recv.at[a, CHUNKS - 1],
            near_as_onward[a],
        )

    pieces = ((1, 0, chip_rows), (0, 0, LEFT), (0, LEFT, chip_rows - LEFT))

    def piece(i, z):
        swap, first, count = pieces[i]
        owner = 1 - z if swap else z
        return owner * chip_rows + first, count

    def zero_copy(i):
        first, count = piece(i, 1 - z_lo)
        at = pl.ds(pl.multiple_of(first, BLK), count)
        far = i == 2
        return remote(
            hops.at[(1 - side[0]) if far else side[0], 0, at, :], raw.at[0, core, at, :],
            zero_send.at[i], zero_recv.at[i], near_same if far else across_same,
        )

    def zero_in(i):
        first, count = piece(i, z_lo)
        at = pl.ds(pl.multiple_of(first, BLK), count)
        return remote(
            hops.at[side[0], 0, at, :], raw.at[0, core, at, :],
            zero_send.at[i], zero_recv.at[i], near_same if i == 2 else across_same,
        )

    def zero_on(i, source):
        first, count = piece(i, z_lo)
        at = pl.ds(pl.multiple_of(first, BLK), count)
        return remote(
            raw.at[0, source, at, :], raw.at[0, source, at, :], zero_send.at[3 + i], zero_recv.at[3 + i], sibling
        )

    def zero_take(i):
        zero_in(i).wait_recv()
        zero_on(i, core).start()
        first, count = piece(i, z_lo)
        mask(0, 5, core, 1 - z_lo, first // BLK, count // BLK)

    def zero_rest(i):
        zero_on(i, 1 - core).wait_recv()
        first, count = piece(i, z_lo)
        mask(0, 5, 1 - core, 1 - z_lo, first // BLK, count // BLK)

    ops = [remote(h_imp, weights.at[:, slot_rows(0, core)], op_send.at[0], op_recv.at[0], sibling)]
    for level in range(1, 5):
        ops.append(
            remote(
                hops.at[side[level], level], raw.at[level, core], op_send.at[level], op_recv.at[level], sibling
            )
        )

    zero_copy(0).start()
    zero_copy(1).start()

    def send(j):
        for q in range(2):
            for a in range(3):
                near_copy(a, j, q, core).start()
        pair_copy(j, core).start()

    send(0)
    zero_copy(2).start()
    for a in range(2):
        for q in range(2):
            early_copy(a, q, core).start()
    for copy in ops:
        copy.start()
    pl.loop(1, CHUNKS)(send)

    def mask(level, slot, q, from_z, first, count):
        def block(p, carry):
            sign = (1 - 2 * signs[level, 0, first + p]).astype(jnp.float32)
            at = pl.ds(pl.multiple_of((first + p) * BLK, BLK), BLK)
            for k in range(rows // BLK):
                keep = patterns[side[level], level, first + p, from_z * 4 + q * 2 + k].astype(jnp.float32)
                factor = jnp.full((BLK, BLK), keep * sign, jnp.float32).astype(jnp.bfloat16)
                to = pl.ds(pl.multiple_of(slot * chip_rows + q * rows + k * BLK, BLK), BLK)
                weights[at, to] = raw[level, q, at, k * BLK : (k + 1) * BLK] * factor
            return carry

        lax.fori_loop(0, count, block, 0)

    def forward(j):
        for a in range(2):
            near_wait(a, j)
            pass_copy(a, j).start()

    def product(z, q, j):
        at = pl.ds(pl.multiple_of(z * chip_rows + q * rows, rows), rows)
        return jnp.dot(weights[at, :], amps[j], preferred_element_type=jnp.float32)

    def compute(j):
        own_copy(j).wait()
        pair_copy(j, core).wait_recv()
        near_wait(2, j)

        @pl.when(j == CHUNKS - 1)
        def _():
            for a in range(2):
                near_wait(a, j)

        for a in range(2):
            pass_copy(a, j).wait_recv()
        for q in range(2):
            value = product(1 - z_lo, q, j)
            most = jnp.maximum(jnp.max(jnp.abs(value), axis=0, keepdims=True), LEAST)
            scales[j, q] = most * (1.0 / TOP)
            coded[j, q] = jnp.round(value * (TOP / most)).astype(jnp.int32).astype(jnp.int16)
            for copy in sum_copy(j, q, core):
                copy.start()

    def compute_own(j):
        stage[j] = product(z_lo, 1 - core, j)
        kept_copy(j, core).start()
        kept[j, core] = product(z_lo, core, j)

    def finish(j):
        kept_copy(j, core).wait_recv()
        e = energy[0]
        for q in range(2):
            for copy in sum_copy(j, q, q):
                copy.wait_recv()
            at = columns(q, j)
            out[:, at] = (
                kept[j, q]
                + coded_in[j, q].astype(jnp.int32).astype(jnp.float32) * scales_in[j, q]
                + e * local[:, at].astype(jnp.float32)
            )

    for copy in small:
        copy.wait()
    for level in range(1, 5):
        mats[level].wait()
        mask(level, level, core, z_lo, 0, 8)
    forward(0)
    for level in range(1, 5):
        ops[level].wait_recv()
        mask(level, level, 1 - core, z_lo, 0, 8)
    mats[0].wait()
    ops[0].wait_recv()
    for j in range(1, AHEAD):
        forward(j)
    zero_take(0)
    for a in range(2):
        for q in range(2):
            early_copy(a, q, q).wait_recv()
        early_pass(a).start()
    zero_rest(0)

    @pl.loop(0, CHUNKS)
    def _(step):
        @pl.when(step + AHEAD < CHUNKS - 1)
        def _():
            forward(step + AHEAD)

        @pl.when(step >= BEHIND)
        def _():
            finish(step - BEHIND)

        compute(step)

        @pl.when(step == 0)
        def _():
            zero_take(1)
            zero_take(2)

        @pl.when(step == 1)
        def _():
            zero_rest(1)
            zero_rest(2)

        @pl.when((step >= 1) & (step <= CHUNKS - LATE))
        def _():
            compute_own(step - 1)


    pl.loop(CHUNKS - LATE, CHUNKS)(compute_own)
    pl.loop(CHUNKS - BEHIND, CHUNKS)(finish)

    for copy in ops:
        copy.wait_send()
    for i in range(3):
        zero_copy(i).wait_send()
        zero_on(i, core).wait_send()
    for a in range(2):
        for q in range(2):
            early_copy(a, q, core).wait_send()

    @pl.loop(0, CHUNKS)
    def _(j):
        for q in range(2):
            for a in range(3):
                near_copy(a, j, q, core).wait_send()
            for copy in sum_copy(j, q, core):
                copy.wait_send()
        for a in range(2):
            pass_copy(a, j).wait_send()
        pair_copy(j, core).wait_send()
        kept_copy(j, core).wait_send()


def per_device(psi, h_imp, hops, patterns, signs, bath_energy):
    here = psi[0]
    rows, rest = here.shape
    imps = h_imp.shape[0]
    width = rest // 2 // CHUNKS
    n = CHUNKS
    dma = pltpu.SemaphoreType.DMA
    anywhere = pl.BlockSpec(memory_space=pltpu.HBM)
    scalar = pl.BlockSpec(memory_space=pltpu.SMEM)
    operands = [pltpu.with_memory_space_constraint(x, pltpu.HBM) for x in (here, h_imp, hops, patterns, signs)]
    applied = pl.pallas_call(
        kernel,
        out_shape=pltpu.VMEM((rows, rest), jnp.float32),
        in_specs=[anywhere] * 5 + [scalar],
        out_specs=pl.BlockSpec(memory_space=pltpu.VMEM),
        scratch_shapes=[
            pltpu.VMEM((5, 2, imps, rows), jnp.bfloat16),
            pltpu.VMEM((imps, 12 * rows), jnp.bfloat16),
            pltpu.VMEM((n, 12 * rows, width), jnp.bfloat16),
            pltpu.VMEM((rows, rest), jnp.bfloat16),
            pltpu.VMEM((n, 2, rows, width), jnp.float32),
            pltpu.VMEM((n, rows, width), jnp.float32),
            pltpu.VMEM((n, 2, rows, width), jnp.int16),
            pltpu.VMEM((n, 2, 1, width), jnp.float32),
            pltpu.VMEM((n, 2, rows, width), jnp.int16),
            pltpu.VMEM((n, 2, 1, width), jnp.float32),
            pltpu.VMEM((2, 2 * rows, width), jnp.bfloat16),
            pltpu.SMEM(patterns.shape, jnp.int32),
            pltpu.SMEM(signs.shape, jnp.int32),
            dma((n,)), dma((5,)), dma((3,)),
            dma((3, n, 2)), dma((3, n, 2)),
            dma((n,)), dma((n,)),
            dma((2, n)), dma((2, n)),
            dma((n, 2, 2)), dma((n, 2, 2)),
            dma((n,)), dma((n,)),
            dma((5,)), dma((5,)),
            dma((6,)), dma((6,)),
            dma((2, 2)), dma((2, 2)),
        ],
        compiler_params=pltpu.CompilerParams(
            collective_id=0, has_side_effects=True, vmem_limit_bytes=50 * 1024 * 1024
        ),
    )(*operands, bath_energy)
    return applied[None]


def solution(mesh):
    placed = (
        P("bath", "imp", None),
        P(None, "imp"),
        P(None, None, None, "imp"),
        P(),
        P(None, "bath", None),
        P("bath"),
    )
    return jax.shard_map(
        per_device, mesh=mesh, in_specs=placed, out_specs=P("bath", "imp", None), check_vma=False
    )
```
